32 devices in a mesh: tm: 4 (over z), sub: 8 (over y, x, core).
Axes of the slice: x: 2, y: 2, z: 4, core: 2. Of those that a mesh axis runs over, the one named last changes fastest.
Arguments:
- starts: float32 [4, 8, 16, 1024], P('tm', 'sub'), may hold values from -6 to 6
- inverses: float32 [8, 1024, 1024], P('sub')
- retain: float32 [8, 1024], P('sub'), may hold values from 0.4 to 1.1
- sources: float32 [8, 16, 1024], P('sub'), may hold values from -4 to 4
- coarse_decay: float32 [8, 1024], P('sub'), may hold values from 0.88 to 0.995
- admittance: float32 [8, 8], P('sub'), may hold values from 0.2 to 0.6
- partner: int32 [8, 8], P('sub'), may hold values from 0 to 63, as said below
- line_delay: int32 [8, 8], P('sub'), may hold values from 2 to 5, as said below
- line_live: int32 [8, 8], P('sub'), may hold values from 0 to 1, as said below
- term_block: int32 [8, 8], P('sub'), may hold values from 0 to 127, as said below
Outputs:
- ends: float32 [4, 8, 16, 1024], P('tm', 'sub')
The draws below stay inside these ranges and needn't reach their ends.
Inputs may be any that keep to these rules, and one draw needn't show every extreme that they name: Slots are paired: partner[i] = k exactly when partner[k] = i. A slot may be its own partner; such a slot is out of service. Of the slots of one index d of sub (its 1 subnetworks), exactly 2 are their own partners, and the others have partners on exactly 3 other indices, 2 slots on each and none elsewhere; these indices are d + 4 and pairs d + s and d - s modulo the number of indices. `line_delay`: paired slots have equal delays. `line_live`: paired slots are both in service or both not. `term_block`: the slots of one subnetwork have distinct blocks.
All inputs are finite; a program needn't handle non-finite values.
Results may differ from the reference program's by a relative error of at most 0.0001.
Values sent between devices are 32-bit elements; how exact they have to be, the bound alone decides.
No kernel may reach another device: no remote copies, remote signals or barrier semaphores. Data moves between devices by JAX's collectives and lax.ppermute only.
A program may use at most 64 MiB of HBM per device.

```python
import math
import jax
import jax.numpy as jnp
from jax import lax

NODES = 1024
TERM = 8
LINES = 8
DMIN = 2
DMAX = 5
FINE = 4
SUB_DEV = 1
COLS = 16
SLICES = 4
SUBNETS = 8
NBLK = 128


def pairing(key):
    slots_dev = SUB_DEV * LINES
    devices_sub = SUBNETS // SUB_DEV
    half_way = devices_sub // 2
    capacity = max(1, 2 * slots_dev // devices_sub)
    groups = slots_dev // capacity
    paired_count = (groups - 2) // 2
    others = 2 + jax.random.permutation(jax.random.fold_in(key, 10), half_way - 2)[:paired_count - 1]
    shift_set = jnp.concatenate([jnp.ones((1,), jnp.int32), others.astype(jnp.int32)])
    perm_keys = jax.random.split(jax.random.fold_in(key, 11), devices_sub)
    placement = jax.vmap(lambda single: jax.random.permutation(single, slots_dev))(perm_keys).astype(jnp.int32)
    canonical = jnp.argsort(placement, axis=1).astype(jnp.int32)
    device_ids = jnp.arange(devices_sub, dtype=jnp.int32)[:, None]
    group_of = canonical // capacity
    paired_group = jnp.maximum(group_of - 2, 0)
    forward = paired_group % 2 == 0
    shift_each = shift_set[jnp.minimum(paired_group // 2, paired_count - 1)]
    pm_dev = jnp.where(forward, (device_ids + shift_each) % devices_sub, (device_ids - shift_each) % devices_sub)
    pm_canon = jnp.where(forward, canonical + capacity, canonical - capacity)
    peer_dev = jnp.where(group_of == 0, (device_ids + half_way) % devices_sub, jnp.where(group_of == 1, device_ids, pm_dev))
    peer_canon = jnp.where(group_of <= 1, canonical, pm_canon)
    mate = peer_dev * slots_dev + placement[peer_dev, peer_canon]
    mate = mate.reshape(-1).astype(jnp.int32)
    group_flat = group_of.reshape(-1)
    slots_all = SUBNETS * LINES
    own = jnp.arange(slots_all, dtype=jnp.int32)
    pair_key = jnp.minimum(own, mate)
    delays = jax.random.randint(jax.random.fold_in(key, 12), (slots_all,), DMIN, DMAX + 1).astype(jnp.int32)
    second = jnp.where(mate[0] == 1, 2, 1).astype(jnp.int32)
    second_key = jnp.minimum(second, mate[second])
    delays = delays.at[0].set(DMAX)
    delays = delays.at[second_key].set(DMIN)
    service = (jax.random.randint(jax.random.fold_in(key, 13), (slots_all,), 0, 4) > 0).astype(jnp.int32)
    service = service[pair_key]
    forced = (group_flat == 0) | (group_flat == 2) | (group_flat == 3)
    service = jnp.where(group_flat == 1, 0, jnp.where(forced, 1, service)).astype(jnp.int32)
    return (mate, delays[pair_key], service)


def draw_partner(key, part):
    return pairing(key)[0].reshape(SUBNETS, LINES).astype(jnp.int32)


def draw_line_delay(key, part):
    return pairing(key)[1].reshape(SUBNETS, LINES).astype(jnp.int32)


def draw_line_live(key, part):
    return pairing(key)[2].reshape(SUBNETS, LINES).astype(jnp.int32)


def draw_term_block(key, part):
    keys = jax.random.split(jax.random.fold_in(key, 14), SUBNETS)
    chosen = jax.vmap(lambda single: jax.random.permutation(single, NBLK)[:LINES])(keys)
    return chosen.astype(jnp.int32)


def draw_inverses(key, part):
    diagonal = 0.45 + 0.2 * jax.random.uniform(jax.random.fold_in(key, 21), (SUBNETS, NODES), jnp.float32)
    spread = jax.random.normal(jax.random.fold_in(key, 22), (SUBNETS, NODES, NODES), jnp.float32)
    spread = spread * (0.3 / NODES ** 0.5)
    return spread + diagonal[:, :, None] * jnp.eye(NODES, dtype=jnp.float32)[None]


def levels(stream_key, extent, cuts, low, high):
    gain, own = 1.0, jax.random.fold_in(stream_key, 6)
    for axis_at, shards_of in cuts:
        heights = jnp.exp(jax.random.uniform(jax.random.fold_in(own, axis_at), (shards_of,), jnp.float32, low / len(cuts), high / len(cuts)))
        gain = gain * jnp.repeat(heights, extent[axis_at] // shards_of).reshape([-1 if axis == axis_at else 1 for axis in range(len(extent))])
    return gain


def normal_values(own_key, extent, width, limit, shards=(), held_as=jnp.bfloat16):
    factor_of = levels(own_key, extent, shards, -0.22, 0.18) if shards else 1.0
    array = jax.random.normal(own_key, extent, jnp.float32) * width * factor_of
    return jnp.minimum(jnp.maximum(array, -limit), limit).astype(held_as)


def setup_inputs(seed: int = 0) -> dict:
    key_list = jax.random.split(jax.random.key(seed), 11)
    return {
        "starts": normal_values(key_list[0], (SLICES, SUBNETS, COLS, NODES), 1.0, 6.0, ((0, 4), (1, 8)), jnp.float32),
        "inverses": draw_inverses(jax.random.fold_in(key_list[10], 71), 0),
        "retain": jnp.clip(jnp.exp(math.log(1.1) - 1.011601 * jax.random.uniform(key_list[2], (SUBNETS, NODES), jnp.float32) ** levels(key_list[2], (SUBNETS, NODES), ((0, 8),), -0.2, 0.2)), 0.4, 1.1),
        "sources": normal_values(key_list[3], (SUBNETS, COLS, NODES), 0.5, 4.0, ((0, 8),), jnp.float32),
        "coarse_decay": jnp.clip(jnp.exp(math.log(0.995) - 0.12282084 * jax.random.uniform(key_list[4], (SUBNETS, NODES), jnp.float32) ** levels(key_list[4], (SUBNETS, NODES), ((0, 8),), -0.2, 0.2)), 0.88, 0.995),
        "admittance": jnp.clip(jnp.exp(math.log(0.6) - 1.0986123 * jax.random.uniform(key_list[5], (SUBNETS, LINES), jnp.float32) ** levels(key_list[5], (SUBNETS, LINES), ((0, 8),), -0.2, 0.2)), 0.2, 0.6),
        "partner": draw_partner(jax.random.fold_in(key_list[10], 71), 0),
        "line_delay": draw_line_delay(jax.random.fold_in(key_list[10], 71), 0),
        "line_live": draw_line_live(jax.random.fold_in(key_list[10], 71), 0),
        "term_block": draw_term_block(jax.random.fold_in(key_list[10], 71), 0),
    }


def terminals(state, term_block):
    grouped = state.reshape(state.shape[0], state.shape[1], state.shape[2], state.shape[3] // TERM, TERM)
    target = (state.shape[0], state.shape[1], state.shape[2], term_block.shape[1], TERM)
    picked = jnp.take_along_axis(grouped, jnp.broadcast_to(term_block[None, :, None, :, None], target), axis=3)
    picked = jnp.transpose(picked, (1, 3, 0, 2, 4))
    return picked.reshape(picked.shape[0] * picked.shape[1], picked.shape[2], picked.shape[3] * TERM)


def inject(collected, partner, line_delay, line_live, admittance, term_block, step, state):
    reach = jnp.maximum(step + 1 - line_delay, 0).reshape(-1).astype(jnp.int32)
    stacked = jnp.concatenate(collected, axis=0)
    everyone = collected[0].shape[0]
    row_index = (reach * everyone + partner.reshape(-1)).astype(jnp.int32)
    far_values = stacked[row_index]
    far_values = far_values.reshape(term_block.shape[0], term_block.shape[1], state.shape[0], state.shape[2], TERM)
    weights = admittance * line_live.astype(jnp.float32)
    far_values = far_values * weights[:, :, None, None, None]
    blocks_here = jnp.arange(state.shape[3] // TERM, dtype=jnp.int32)
    onehot = (term_block[:, :, None] == blocks_here[None, None, :]).astype(jnp.float32)
    placed = jnp.einsum('plsct,plb->spcbt', far_values, onehot, precision=lax.Precision.HIGHEST)
    return placed.reshape(state.shape)


def advance(state, inverses, retain, sources, injected):
    driven = retain[None, :, None, :] * state + sources[None] + injected
    return jnp.einsum('spcm,pnm->spcn', driven, inverses, precision=lax.Precision.HIGHEST, preferred_element_type=jnp.float32)


def reference(starts, inverses, retain, sources, coarse_decay, admittance, partner, line_delay, line_live, term_block):
    state = starts
    collected = [terminals(state, term_block)]
    for step in range(FINE):
        injected = inject(collected, partner, line_delay, line_live, admittance, term_block, step, state)
        state = advance(state, inverses, retain, sources, injected)
        if step + 1 <= FINE - DMIN:
            collected.append(terminals(state, term_block))
    offsets = state - coarse_decay[None, :, None, :] * starts
    current = starts[0]
    finals = []
    for slice_index in range(SLICES):
        current = coarse_decay[:, None, :] * current + offsets[slice_index]
        finals.append(current)
    return jnp.stack(finals)
```

```python
import functools

import jax
import jax.numpy as jnp
from jax import lax
from jax.experimental import pallas as pl
from jax.experimental.pallas import tpu as pltpu
from jax.sharding import PartitionSpec as P

TERM = 8
CHUNKS = 4

f32 = jnp.float32
bf16 = jnp.bfloat16
ROWS_BY_ROWS = (((1,), (1,)), ((), ()))


def split(value):
    high = value.astype(bf16)
    return high, (value - high.astype(f32)).astype(bf16)


def stacked(value):
    return jnp.concatenate(split(value), axis=0)


def folded(value):
    half = value.shape[0] // 2
    return value[:half] + value[half:]


def times_rows(left, high, low):
    return lax.dot_general(left, high, ROWS_BY_ROWS, preferred_element_type=f32) + lax.dot_general(
        left, low, ROWS_BY_ROWS, preferred_element_type=f32
    )


def times(left, right):
    return jnp.dot(left, right, preferred_element_type=f32)


def slot_lanes(lines, width, read):
    slot = lax.broadcasted_iota(jnp.int32, (1, width), 1) // TERM % lines
    row = jnp.full((1, width), read(0))
    for line in range(1, lines):
        row = jnp.where(slot == line, read(line), row)
    return row


def first_kernel(
    block_ref, partner_ref, live_ref, admittance_ref,
    start_ref, source_ref, retain_ref, inverse_ref,
    package_ref, moved_ref, high_ref, low_ref,
    held, picked, arrived,
):
    cols, nodes = start_ref.shape
    lines = block_ref.shape[1]
    points = lines * TERM
    depth = nodes // CHUNKS
    copies = []
    for part in range(CHUNKS):
        rows = pl.ds(part * depth, depth)
        copies.append(
            pltpu.make_async_copy(inverse_ref.at[rows], held.at[rows], arrived.at[part])
        )
        copies[-1].start()
    offset = lax.broadcasted_iota(jnp.int32, (TERM, nodes), 1) - lax.broadcasted_iota(
        jnp.int32, (TERM, nodes), 0
    )
    chosen = jnp.concatenate(
        [(offset == block_ref[0, line] * TERM).astype(f32) for line in range(lines)], axis=0
    ).astype(bf16)
    retain = retain_ref[...]
    source = source_ref[...]
    start = start_ref[...]
    left = jnp.concatenate([stacked(retain * start + source), chosen], axis=0)
    for part in range(CHUNKS):
        copies[part].wait()
        rows = pl.ds(part * depth, depth)
        high, low = split(held[rows, :])
        high_ref[rows, :] = high
        low_ref[rows, :] = low
        out = times_rows(left, high, low)
        moved_ref[:cols, rows] = folded(out[: 2 * cols])
        moved_ref[cols:, rows] = out[2 * cols :]
    picked[:points, :] = jnp.zeros((points, nodes), f32)
    for line in range(lines):
        picked[points + line * TERM : points + (line + 1) * TERM, :] = held[
            pl.ds(pl.multiple_of(block_ref[0, line] * TERM, TERM), TERM), :
        ]
    moved = moved_ref[...]
    driven = jnp.concatenate(
        [retain * moved[:cols] + source, retain * moved[cols:]], axis=0
    )
    second = folded(times_rows(stacked(driven), *split(picked[...])))
    everything = jnp.concatenate([start, moved], axis=0)
    twice = jnp.concatenate([chosen, chosen], axis=0)
    firsts = folded(
        lax.dot_general(stacked(everything), twice, ROWS_BY_ROWS, preferred_element_type=f32)
    )
    lane = lax.broadcasted_iota(jnp.int32, (cols, 2 * points), 1)
    table = slot_lanes(lines, 2 * points, lambda line: partner_ref[0, line] * TERM)
    table = (table + lax.broadcasted_iota(jnp.int32, table.shape, 1) % TERM).astype(f32)
    package_ref[:cols, :] = jnp.where(lane < points, firsts[:cols], table)
    package_ref[cols : 2 * cols, :] = jnp.where(
        lane < points, firsts[cols : 2 * cols], second[:cols]
    )
    answers = firsts[2 * cols :] + second[cols:]
    for line in range(lines):
        weight = admittance_ref[0, line] * live_ref[0, line].astype(f32)
        rows = slice(line * TERM, (line + 1) * TERM)
        package_ref[2 * cols + line * TERM : 2 * cols + (line + 1) * TERM, :] = (
            weight * answers[rows]
        )


def middle_kernel(
    moved_ref, high_ref, low_ref, start_ref, source_ref, retain_ref, decay_ref,
    base_ref, reply_high_ref, reply_low_ref,
):
    cols, nodes = start_ref.shape
    points = moved_ref.shape[0] - cols
    retain = retain_ref[...]
    source = source_ref[...]
    state = moved_ref[...]
    replies = [state[cols:]]
    for _ in range(3):
        driven = jnp.concatenate(
            [retain * state[:cols] + source, retain * state[cols:]], axis=0
        )
        state = folded(times_rows(stacked(driven), high_ref[...], low_ref[...]))
        replies.append(state[cols:])
    kept = decay_ref[...] * start_ref[...]
    offset = state[:cols] - kept
    leading = lax.axis_index("tm") == 0
    base_ref[...] = jnp.where(leading, offset + kept, offset)
    reply = jnp.concatenate(
        [replies[3] + replies[2], jnp.zeros((points, nodes), f32), replies[1], replies[0]], axis=0
    )
    reply_high_ref[...], reply_low_ref[...] = split(reply)


def last_kernel(
    count, partner_ref, delay_ref, live_ref, admittance_ref, here_ref, there_ref, base_ref,
    reply_high_ref, reply_low_ref, out_ref,
):
    cols = base_ref.shape[0]
    lines = partner_ref.shape[1]
    points = lines * TERM
    width = 2 * points
    mine = lax.axis_index("sub")
    lane = lax.broadcasted_iota(jnp.int32, (cols, width), 1)
    pairs = []
    tables = []
    for pair in range(count // 2):
        even = here_ref[pair, :cols, :]
        odd = pltpu.roll(there_ref[pair, :cols, :], points, 1)
        pairs.append(jnp.where(lane < points, even, odd))
        tables.append(
            jnp.where(lane < points, pltpu.roll(even, points, 1), pltpu.roll(odd, points, 1))[:1]
        )
    snapshot = jnp.concatenate(pairs, axis=1)
    table = jnp.concatenate(tables, axis=1).astype(jnp.int32) ^ (mine * points)
    total = count * points
    route = (lax.broadcasted_iota(jnp.int32, (total, total), 0) == table).astype(f32).astype(bf16)
    far = folded(times(stacked(snapshot), route))
    later = []
    for pair in range(count // 2):
        both = far[:, pair * width : (pair + 1) * width]
        rows = jnp.concatenate(
            [stacked(jnp.where(lane < points, both, 0.0)), stacked(jnp.where(lane < points, 0.0, both))],
            axis=0,
        )
        answers = jnp.concatenate(
            [here_ref[pair, 2 * cols :, :], there_ref[pair, 2 * cols :, :]], axis=0
        )
        high, low = split(answers)
        sums = times(rows, high) + times(rows, low)
        later.append(here_ref[pair, cols : 2 * cols, :] + folded(sums[: 2 * cols]))
        later.append(there_ref[pair, cols : 2 * cols, :] + folded(sums[2 * cols :]))
    known = jnp.concatenate(later + [snapshot], axis=1)
    delay = slot_lanes(lines, width, lambda line: delay_ref[0, line])
    slot = slot_lanes(lines, width, lambda line: partner_ref[0, line])
    weight = slot_lanes(
        lines, width, lambda line: admittance_ref[0, line] * live_ref[0, line].astype(f32)
    )
    index = lax.broadcasted_iota(jnp.int32, (1, width), 1)
    source = (slot * TERM + index % TERM) ^ (mine * points)
    late = index >= points
    within = source % points
    start = source // points * width + within
    wanted = jnp.where(
        late,
        jnp.where(delay == 2, start + points, jnp.where(delay == 3, start, count * width + source)),
        jnp.where(delay == 2, start, count * width + source),
    )
    pick = (lax.broadcasted_iota(jnp.int32, (known.shape[1], width), 0) == wanted)
    chosen = folded(times(stacked(known), pick.astype(f32).astype(bf16)))
    first = jnp.where(lane < points, far[:, :width], 0.0)
    rows = stacked(jnp.concatenate([weight * first, weight * chosen], axis=1))
    out_ref[...] = base_ref[...] + folded(
        times(rows, reply_high_ref[...]) + times(rows, reply_low_ref[...])
    )


def combine_kernel(count, decay_ref, *refs):
    parts, out_ref = refs[:count], refs[count]
    mine = lax.axis_index("tm")
    decay = decay_ref[...]
    loaded = [part[...] for part in parts]
    total = jnp.zeros_like(loaded[0])
    for turn in range(count):
        value = loaded[0]
        for place in range(1, count):
            value = jnp.where((mine ^ turn) == place, loaded[place], value)
        total = jnp.where(turn <= mine, decay * total + value, total)
    out_ref[...] = total


def exchanged(value, axis, count, flip):
    return lax.ppermute(value, axis, [(source, source ^ flip) for source in range(count)])


VMEM = pl.BlockSpec(memory_space=pltpu.VMEM)
SMEM = pl.BlockSpec(memory_space=pltpu.SMEM)
ANY = pl.BlockSpec(memory_space=pl.ANY)


def shards(
    times_count, subs, starts, inverses, retain, sources, coarse_decay, admittance, partner,
    line_delay, line_live, term_block,
):
    cols, nodes = starts.shape[2:]
    points = partner.shape[1] * TERM
    width = 2 * points
    start = starts.reshape(cols, nodes)
    source = sources.reshape(cols, nodes)
    inverse = inverses.reshape(nodes, nodes)
    shape = jax.ShapeDtypeStruct
    package, moved, high, low = pl.pallas_call(
        first_kernel,
        out_shape=(
            shape((2 * cols + points, width), f32),
            shape((cols + points, nodes), f32),
            shape((nodes, nodes), bf16),
            shape((nodes, nodes), bf16),
        ),
        in_specs=[SMEM] * 4 + [VMEM] * 3 + [ANY],
        out_specs=(VMEM,) * 4,
        scratch_shapes=[
            pltpu.VMEM((nodes, nodes), f32),
            pltpu.VMEM((width, nodes), f32),
            pltpu.SemaphoreType.DMA((CHUNKS,)),
        ],
        compiler_params=pltpu.CompilerParams(vmem_limit_bytes=24 << 20),
        name="first",
    )(term_block, partner, line_live, admittance, start, source, retain, inverse)

    base, reply_high, reply_low = pl.pallas_call(
        middle_kernel,
        out_shape=(
            shape((cols, nodes), f32),
            shape((4 * points, nodes), bf16),
            shape((4 * points, nodes), bf16),
        ),
        in_specs=[VMEM] * 7,
        out_specs=(VMEM,) * 3,
        compiler_params=pltpu.CompilerParams(vmem_limit_bytes=24 << 20),
        name="middle",
    )(moved, high, low, start, source, retain, coarse_decay)

    here = jnp.stack(
        [package] + [exchanged(package, "sub", subs, flip) for flip in range(2, subs, 2)]
    )
    there = exchanged(here, "sub", subs, 1)

    value = pl.pallas_call(
        functools.partial(last_kernel, subs),
        out_shape=shape((cols, nodes), f32),
        in_specs=[SMEM] * 4 + [VMEM] * 5,
        out_specs=VMEM,
        compiler_params=pltpu.CompilerParams(vmem_limit_bytes=40 << 20),
        name="last",
    )(partner, line_delay, line_live, admittance, here, there, base, reply_high, reply_low)

    parts = [value] + [
        exchanged(value, "tm", times_count, flip) for flip in range(1, times_count)
    ]
    ends = pl.pallas_call(
        functools.partial(combine_kernel, times_count),
        out_shape=shape((cols, nodes), f32),
        in_specs=[VMEM] * (1 + times_count),
        out_specs=VMEM,
        compiler_params=pltpu.CompilerParams(vmem_limit_bytes=8 << 20),
        name="combine",
    )(coarse_decay, *parts)
    return ends.reshape(starts.shape)


def solution(mesh):
    return jax.shard_map(
        functools.partial(shards, mesh.shape["tm"], mesh.shape["sub"]),
        mesh=mesh,
        in_specs=(
            P("tm", "sub", None, None),
            P("sub", None, None),
            P("sub", None),
            P("sub", None, None),
            P("sub", None),
            P("sub", None),
            P("sub", None),
            P("sub", None),
            P("sub", None),
            P("sub", None),
        ),
        out_specs=P("tm", "sub", None, None),
        check_vma=False,
    )
```

```python
import functools

import jax
import jax.numpy as jnp
from jax import lax
from jax.experimental import pallas as pl
from jax.experimental.pallas import tpu as pltpu
from jax.sharding import PartitionSpec as P

TERM = 8
CHUNKS = 4

f32 = jnp.float32
bf16 = jnp.bfloat16
ROWS_BY_ROWS = (((1,), (1,)), ((), ()))


def split(value):
    high = value.astype(bf16)
    return high, (value - high.astype(f32)).astype(bf16)


def stacked(value):
    return jnp.concatenate(split(value), axis=0)


def folded(value):
    half = value.shape[0] // 2
    return value[:half] + value[half:]


def times_rows(left, high, low):
    return lax.dot_general(left, high, ROWS_BY_ROWS, preferred_element_type=f32) + lax.dot_general(
        left, low, ROWS_BY_ROWS, preferred_element_type=f32
    )


def times(left, right):
    return jnp.dot(left, right, preferred_element_type=f32)


def slot_lanes(lines, width, read):
    slot = lax.broadcasted_iota(jnp.int32, (1, width), 1) // TERM % lines
    row = jnp.full((1, width), read(0))
    for line in range(1, lines):
        row = jnp.where(slot == line, read(line), row)
    return row


def prepare_kernel(
    block_hbm, partner_hbm, live_hbm, admittance_hbm, source_hbm, retain_hbm, inverse_hbm,
    high_ref, low_ref, probe_high_ref, probe_low_ref, answer_ref, shift_ref,
    block_ref, partner_ref, live_ref, admittance_ref, source_ref, retain_ref, held, picked,
    landed, arrived, fetched,
):
    nodes = inverse_hbm.shape[0]
    lines = block_ref.shape[1]
    points = lines * TERM
    depth = nodes // CHUNKS
    small = [
        pltpu.make_async_copy(source, target, landed.at[place])
        for place, (source, target) in enumerate(
            [
                (block_hbm, block_ref),
                (partner_hbm, partner_ref),
                (live_hbm, live_ref),
                (admittance_hbm, admittance_ref),
                (source_hbm, source_ref),
                (retain_hbm, retain_ref),
            ]
        )
    ]
    for copy in small:
        copy.start()
    copies = []
    for part in range(CHUNKS):
        rows = pl.ds(part * depth, depth)
        copies.append(
            pltpu.make_async_copy(inverse_hbm.at[rows], held.at[rows], arrived.at[part])
        )
        copies[-1].start()
    small[0].wait()
    rows_wanted = []
    for line in range(lines):
        rows_wanted.append(
            pltpu.make_async_copy(
                inverse_hbm.at[pl.ds(pl.multiple_of(block_ref[0, line] * TERM, TERM), TERM)],
                picked.at[pl.ds(line * TERM, TERM)],
                fetched.at[line],
            )
        )
        rows_wanted[-1].start()
    offset = lax.broadcasted_iota(jnp.int32, (TERM, nodes), 1) - lax.broadcasted_iota(
        jnp.int32, (TERM, nodes), 0
    )
    chosen = jnp.concatenate(
        [(offset == block_ref[0, line] * TERM).astype(f32) for line in range(lines)], axis=0
    ).astype(bf16)
    for copy in small[1:] + rows_wanted:
        copy.wait()
    near = picked[...]
    left = stacked(near * retain_ref[...])
    total = jnp.zeros((2 * points, nodes), f32)
    for part in range(CHUNKS):
        copies[part].wait()
        rows = pl.ds(part * depth, depth)
        high, low = split(held[rows, :])
        high_ref[rows, :] = high
        low_ref[rows, :] = low
        piece = left[:, part * depth : (part + 1) * depth]
        total = total + times(piece, high) + times(piece, low)
    beyond = folded(total)
    near_high, near_low = split(near)
    beyond_high, beyond_low = split(beyond)
    probe_high_ref[:points, :] = chosen
    probe_high_ref[points : 2 * points, :] = jnp.zeros_like(chosen)
    probe_high_ref[2 * points : 3 * points, :] = near_high
    probe_high_ref[3 * points :, :] = beyond_high
    probe_low_ref[: 2 * points, :] = jnp.zeros((2 * points, nodes), bf16)
    probe_low_ref[2 * points : 3 * points, :] = near_low
    probe_low_ref[3 * points :, :] = beyond_low
    blank = jnp.zeros_like(chosen)
    shift_ref[...] = folded(
        times_rows(
            stacked(source_ref[...]),
            jnp.concatenate([blank, near_high], axis=0),
            jnp.concatenate([blank, near_low], axis=0),
        )
    )
    answers = times_rows(chosen, *split(jnp.concatenate([near, near + beyond], axis=0)))
    for line in range(lines):
        weight = admittance_ref[0, line] * live_ref[0, line].astype(f32)
        rows = slice(line * TERM, (line + 1) * TERM)
        answer_ref[rows, :] = weight * answers[rows]
    table = slot_lanes(lines, 2 * points, lambda line: partner_ref[0, line] * TERM)
    table = table + lax.broadcasted_iota(jnp.int32, table.shape, 1) % TERM
    answer_ref[points:, :] = jnp.broadcast_to(table.astype(f32), (TERM, 2 * points))


def package_kernel(count, source_ref, retain_ref, probe_high_ref, probe_low_ref, answer_ref, shift_ref, *refs):
    starts, package_ref = refs[:count], refs[count]
    cols, width = shift_ref.shape
    start = jnp.concatenate([ref[...] for ref in starts], axis=0)
    source = jnp.concatenate([source_ref[...]] * count, axis=0)
    driven = retain_ref[...] * start + source
    terms = folded(
        lax.dot_general(
            stacked(start), probe_high_ref[:width, :], ROWS_BY_ROWS, preferred_element_type=f32
        )
    )
    later = folded(
        times_rows(stacked(driven), probe_high_ref[width:, :], probe_low_ref[width:, :])
    )
    rows = count * cols
    package_ref[:rows, :] = terms
    package_ref[rows : 2 * rows, :] = later + jnp.concatenate([shift_ref[...]] * count, axis=0)
    package_ref[2 * rows :, :] = answer_ref[...]


def advance_kernel(count, turns, high_ref, low_ref, probe_ref, source_ref, retain_ref, *refs):
    starts = refs[:count]
    state_ref, replies_ref = refs[count:]
    points = probe_ref.shape[0] // 4
    rows = count * source_ref.shape[0]
    retain = retain_ref[...]
    source = jnp.concatenate([source_ref[...]] * count, axis=0)
    start = jnp.concatenate([ref[...] for ref in starts], axis=0)
    high, low = high_ref[...], low_ref[...]
    left = jnp.concatenate([stacked(retain * start + source), probe_ref[:points, :]], axis=0)
    out = times_rows(left, high, low)
    state = jnp.concatenate([folded(out[: 2 * rows]), out[2 * rows :]], axis=0)
    for turn in range(turns):
        replies_ref[turn * points : (turn + 1) * points, :] = state[rows:]
        driven = jnp.concatenate(
            [retain * state[:rows] + source, retain * state[rows:]], axis=0
        )
        state = folded(times_rows(stacked(driven), high, low))
    state_ref[...] = state


def finish_kernel(
    count, high_ref, low_ref, state_ref, replies_ref, source_ref, retain_ref, decay_ref, *refs
):
    starts = refs[:count]
    base_ref, reply_high_ref, reply_low_ref, partial = refs[count:]
    cols, nodes = source_ref.shape
    rows = count * cols
    points = state_ref.shape[0] - rows
    retain = retain_ref[...]
    decay = decay_ref[...]
    source = jnp.concatenate([source_ref[...]] * count, axis=0)
    state = state_ref[...]
    driven = jnp.concatenate([retain * state[:rows] + source, retain * state[rows:]], axis=0)
    final = folded(times_rows(stacked(driven), high_ref[...], low_ref[...]))
    start = jnp.concatenate([ref[...] for ref in starts], axis=0)
    partial[...] = final[:rows] - decay * start
    mine = lax.axis_index("tm")
    first = pl.ds(pl.multiple_of(mine * cols, cols), cols)
    total = partial[first, :]
    seed = starts[0][...]
    for place in range(1, count):
        seed = jnp.where(mine == place, starts[place][...], seed)
    total = total + decay * seed
    for turn in range(1, count):
        value = partial[pl.ds(pl.multiple_of((mine ^ turn) * cols, cols), cols), :]
        total = jnp.where(turn <= mine, decay * total + value, total)
    base_ref[...] = total
    reply = jnp.concatenate(
        [
            final[rows:] + state[rows:],
            jnp.zeros((points, nodes), f32),
            replies_ref[points : 2 * points, :],
            replies_ref[:points, :],
        ],
        axis=0,
    )
    reply_high_ref[...], reply_low_ref[...] = split(reply)


def last_kernel(
    subs, count, partner_ref, delay_ref, live_ref, admittance_ref, here_ref, there_ref, base_ref,
    decay_ref, reply_high_ref, reply_low_ref, out_ref, partial,
):
    cols, nodes = base_ref.shape
    lines = partner_ref.shape[1]
    points = lines * TERM
    width = 2 * points
    rows = count * cols
    mine = lax.axis_index("sub")
    lane = lax.broadcasted_iota(jnp.int32, (rows, width), 1)
    pairs = []
    tables = []
    for pair in range(subs // 2):
        odd = pltpu.roll(there_ref[pair, :rows, :], points, 1)
        pairs.append(jnp.where(lane < points, here_ref[pair, :rows, :], odd))
        tables.append(
            jnp.where(
                lane[:TERM] < points,
                here_ref[pair, 2 * rows + points :, :],
                there_ref[pair, 2 * rows + points :, :],
            )[:1]
        )
    snapshot = jnp.concatenate(pairs, axis=1)
    table = jnp.concatenate(tables, axis=1).astype(jnp.int32) ^ (mine * points)
    total = subs * points
    route = (lax.broadcasted_iota(jnp.int32, (total, total), 0) == table).astype(f32).astype(bf16)
    far = folded(times(stacked(snapshot), route))
    later = []
    for pair in range(subs // 2):
        both = far[:, pair * width : (pair + 1) * width]
        left = jnp.concatenate(
            [
                stacked(jnp.where(lane < points, both, 0.0)),
                stacked(jnp.where(lane < points, 0.0, both)),
            ],
            axis=0,
        )
        answers = jnp.concatenate(
            [
                here_ref[pair, 2 * rows : 2 * rows + points, :],
                there_ref[pair, 2 * rows : 2 * rows + points, :],
            ],
            axis=0,
        )
        high, low = split(answers)
        sums = times(left, high) + times(left, low)
        later.append(here_ref[pair, rows : 2 * rows, :] + folded(sums[: 2 * rows]))
        later.append(there_ref[pair, rows : 2 * rows, :] + folded(sums[2 * rows :]))
    known = jnp.concatenate(later + [snapshot], axis=1)
    delay = slot_lanes(lines, width, lambda line: delay_ref[0, line])
    slot = slot_lanes(lines, width, lambda line: partner_ref[0, line])
    weight = slot_lanes(
        lines, width, lambda line: admittance_ref[0, line] * live_ref[0, line].astype(f32)
    )
    index = lax.broadcasted_iota(jnp.int32, (1, width), 1)
    source = (slot * TERM + index % TERM) ^ (mine * points)
    late = index >= points
    start = source // points * width + source % points
    wanted = jnp.where(
        late,
        jnp.where(delay == 2, start + points, jnp.where(delay == 3, start, subs * width + source)),
        jnp.where(delay == 2, start, subs * width + source),
    )
    pick = lax.broadcasted_iota(jnp.int32, (known.shape[1], width), 0) == wanted
    chosen = folded(times(stacked(known), pick.astype(f32).astype(bf16)))
    first = jnp.where(lane < points, far[:, :width], 0.0)
    left = stacked(jnp.concatenate([weight * first, weight * chosen], axis=1))
    partial[...] = folded(times(left, reply_high_ref[...]) + times(left, reply_low_ref[...]))
    decay = decay_ref[...]
    place = lax.axis_index("tm")
    total = partial[pl.ds(pl.multiple_of(place * cols, cols), cols), :]
    for turn in range(1, count):
        value = partial[pl.ds(pl.multiple_of((place ^ turn) * cols, cols), cols), :]
        total = jnp.where(turn <= place, decay * total + value, total)
    out_ref[...] = base_ref[...] + total


def exchanged(value, axis, count, flip):
    return lax.ppermute(value, axis, [(source, source ^ flip) for source in range(count)])


VMEM = pl.BlockSpec(memory_space=pltpu.VMEM)
SMEM = pl.BlockSpec(memory_space=pltpu.SMEM)
HBM = pl.BlockSpec(memory_space=pltpu.HBM)


def shards(
    slices, subs, starts, inverses, retain, sources, coarse_decay, admittance, partner,
    line_delay, line_live, term_block,
):
    cols, nodes = starts.shape[2:]
    lines = partner.shape[1]
    points = lines * TERM
    width = 2 * points
    rows = slices * cols
    start = starts.reshape(cols, nodes)
    source = sources.reshape(cols, nodes)
    inverse = inverses.reshape(nodes, nodes)
    shape = jax.ShapeDtypeStruct
    begun = [start] + [exchanged(start, "tm", slices, flip) for flip in range(1, slices)]
    high, low, probe_high, probe_low, answer, shift = pl.pallas_call(
        prepare_kernel,
        out_shape=(
            shape((nodes, nodes), bf16),
            shape((nodes, nodes), bf16),
            shape((4 * points, nodes), bf16),
            shape((4 * points, nodes), bf16),
            shape((points + TERM, width), f32),
            shape((cols, width), f32),
        ),
        in_specs=[HBM] * 7,
        out_specs=(VMEM,) * 6,
        scratch_shapes=[
            pltpu.SMEM((1, lines), jnp.int32),
            pltpu.SMEM((1, lines), jnp.int32),
            pltpu.SMEM((1, lines), jnp.int32),
            pltpu.SMEM((1, lines), f32),
            pltpu.VMEM((cols, nodes), f32),
            pltpu.VMEM((1, nodes), f32),
            pltpu.VMEM((nodes, nodes), f32),
            pltpu.VMEM((points, nodes), f32),
            pltpu.SemaphoreType.DMA((6,)),
            pltpu.SemaphoreType.DMA((CHUNKS,)),
            pltpu.SemaphoreType.DMA((lines,)),
        ],
        compiler_params=pltpu.CompilerParams(vmem_limit_bytes=24 << 20),
        name="prepare",
    )(
        *[
            pltpu.with_memory_space_constraint(value, pltpu.HBM)
            for value in (term_block, partner, line_live, admittance, source, retain, inverse)
        ]
    )

    package = pl.pallas_call(
        functools.partial(package_kernel, slices),
        out_shape=shape((2 * rows + points + TERM, width), f32),
        in_specs=[VMEM] * (6 + slices),
        out_specs=VMEM,
        compiler_params=pltpu.CompilerParams(vmem_limit_bytes=16 << 20),
        name="package",
    )(source, retain, probe_high, probe_low, answer, shift, *begun)

    state, replies = pl.pallas_call(
        functools.partial(advance_kernel, slices, 2),
        out_shape=(shape((rows + points, nodes), f32), shape((2 * points, nodes), f32)),
        in_specs=[VMEM] * (5 + slices),
        out_specs=(VMEM,) * 2,
        compiler_params=pltpu.CompilerParams(vmem_limit_bytes=24 << 20),
        cost_estimate=pl.CostEstimate(
            flops=12 * nodes * nodes * 256, bytes_accessed=8 * nodes * nodes, transcendentals=0
        ),
        name="advance",
    )(high, low, probe_high, source, retain, *begun)

    here = jnp.stack(
        [package] + [exchanged(package, "sub", subs, flip) for flip in range(2, subs, 2)]
    )
    here, state = lax.optimization_barrier((here, state))
    there = exchanged(here, "sub", subs, 1)

    base, reply_high, reply_low = pl.pallas_call(
        functools.partial(finish_kernel, slices),
        out_shape=(
            shape((cols, nodes), f32),
            shape((4 * points, nodes), bf16),
            shape((4 * points, nodes), bf16),
        ),
        in_specs=[VMEM] * (7 + slices),
        out_specs=(VMEM,) * 3,
        scratch_shapes=[pltpu.VMEM((rows, nodes), f32)],
        compiler_params=pltpu.CompilerParams(vmem_limit_bytes=24 << 20),
        cost_estimate=pl.CostEstimate(
            flops=4 * nodes * nodes * 256, bytes_accessed=4 * nodes * nodes, transcendentals=0
        ),
        name="finish",
    )(high, low, state, replies, source, retain, coarse_decay, *begun)

    ends = pl.pallas_call(
        functools.partial(last_kernel, subs, slices),
        out_shape=shape((cols, nodes), f32),
        in_specs=[SMEM] * 4 + [VMEM] * 6,
        out_specs=VMEM,
        scratch_shapes=[pltpu.VMEM((rows, nodes), f32)],
        compiler_params=pltpu.CompilerParams(vmem_limit_bytes=40 << 20),
        name="last",
    )(
        partner, line_delay, line_live, admittance, here, there, base, coarse_decay,
        reply_high, reply_low,
    )
    return ends.reshape(starts.shape)


def solution(mesh):
    return jax.shard_map(
        functools.partial(shards, mesh.shape["tm"], mesh.shape["sub"]),
        mesh=mesh,
        in_specs=(
            P("tm", "sub", None, None),
            P("sub", None, None),
            P("sub", None),
            P("sub", None, None),
            P("sub", None),
            P("sub", None),
            P("sub", None),
            P("sub", None),
            P("sub", None),
            P("sub", None),
        ),
        out_specs=P("tm", "sub", None, None),
        check_vma=False,
    )
```

```python
import functools

import jax
import jax.numpy as jnp
from jax import lax
from jax.experimental import pallas as pl
from jax.experimental.pallas import tpu as pltpu
from jax.sharding import PartitionSpec as P

TERM = 8
CHUNKS = 4

f32 = jnp.float32
bf16 = jnp.bfloat16
ROWS_BY_ROWS = (((1,), (1,)), ((), ()))


def split(value):
    high = value.astype(bf16)
    return high, (value - high.astype(f32)).astype(bf16)


def stacked(value):
    return jnp.concatenate(split(value), axis=0)


def folded(value):
    half = value.shape[0] // 2
    return value[:half] + value[half:]


def times_rows(left, high, low):
    return lax.dot_general(left, high, ROWS_BY_ROWS, preferred_element_type=f32) + lax.dot_general(
        left, low, ROWS_BY_ROWS, preferred_element_type=f32
    )


def times(left, right):
    return jnp.dot(left, right, preferred_element_type=f32)


def slot_lanes(lines, width, read):
    slot = lax.broadcasted_iota(jnp.int32, (1, width), 1) // TERM % lines
    row = jnp.full((1, width), read(0))
    for line in range(1, lines):
        row = jnp.where(slot == line, read(line), row)
    return row


def prepare_kernel(
    subs, block_hbm, partner_hbm, delay_hbm, live_hbm, admittance_hbm, source_hbm, retain_hbm,
    inverse_hbm, high_ref, low_ref, probe_high_ref, probe_low_ref, answer_ref, shift_ref, plan_ref,
    block_ref, partner_ref, delay_ref, live_ref, admittance_ref, source_ref, retain_ref, held,
    picked, landed, arrived, fetched,
):
    nodes = inverse_hbm.shape[0]
    lines = block_ref.shape[1]
    points = lines * TERM
    width = 2 * points
    depth = nodes // CHUNKS
    small = [
        pltpu.make_async_copy(source, target, landed.at[place])
        for place, (source, target) in enumerate(
            [
                (block_hbm, block_ref),
                (source_hbm, source_ref),
                (retain_hbm, retain_ref),
                (partner_hbm, partner_ref),
                (delay_hbm, delay_ref),
                (live_hbm, live_ref),
                (admittance_hbm, admittance_ref),
            ]
        )
    ]
    pieces = [pl.ds(part * depth, depth) for part in range(CHUNKS)]
    copies = [
        pltpu.make_async_copy(inverse_hbm.at[rows], held.at[rows], arrived.at[part])
        for part, rows in enumerate(pieces)
    ]
    for copy in small + copies:
        copy.start()
    small[0].wait()
    wanted = [
        pltpu.make_async_copy(
            inverse_hbm.at[pl.ds(pl.multiple_of(block_ref[0, line] * TERM, TERM), TERM)],
            picked.at[pl.ds(line * TERM, TERM)],
            fetched.at[line],
        )
        for line in range(lines)
    ]
    for copy in wanted:
        copy.start()
    offset = lax.broadcasted_iota(jnp.int32, (TERM, nodes), 1) - lax.broadcasted_iota(
        jnp.int32, (TERM, nodes), 0
    )
    chosen = jnp.concatenate(
        [(offset == block_ref[0, line] * TERM).astype(f32) for line in range(lines)], axis=0
    ).astype(bf16)
    probe_high_ref[:points, :] = chosen
    blank = jnp.zeros_like(chosen)
    for copy in small[1:]:
        copy.wait()
    weights = [
        admittance_ref[0, line] * live_ref[0, line].astype(f32) for line in range(lines)
    ]
    index = lax.broadcasted_iota(jnp.int32, (1, width), 1)
    table = slot_lanes(lines, width, lambda line: partner_ref[0, line] * TERM) + index % TERM
    answer_ref[points:, :] = jnp.broadcast_to(table.astype(f32), (TERM, width))
    place = table ^ (lax.axis_index("sub") * points)
    delay = slot_lanes(lines, width, lambda line: delay_ref[0, line])
    begin = place // points * width + place % points
    early = subs * width + place
    target = jnp.where(
        index >= points,
        jnp.where(delay == 2, begin + points, jnp.where(delay == 3, begin, early)),
        jnp.where(delay == 2, begin, early),
    )
    plan_ref[...] = jnp.concatenate(
        [slot_lanes(lines, width, lambda line: weights[line]), target.astype(f32)], axis=0
    )

    def keep(part):
        copies[part].wait()
        high_ref[pieces[part], :], low_ref[pieces[part], :] = split(held[pieces[part], :])

    for part in range(CHUNKS):
        keep(part)
    for copy in wanted:
        copy.wait()
    near = picked[...]
    near_high, near_low = split(near)
    left = stacked(near * retain_ref[...])
    probe_high_ref[points : 2 * points, :] = near_high
    probe_low_ref[:points, :] = near_low
    shift_ref[...] = folded(
        times_rows(
            stacked(source_ref[...]),
            jnp.concatenate([blank, near_high], axis=0),
            jnp.concatenate([blank, near_low], axis=0),
        )
    )
    total = jnp.zeros((2 * points, nodes), f32)
    for part in range(CHUNKS):
        piece = left[:, part * depth : (part + 1) * depth]
        total = total + times(piece, high_ref[pieces[part], :])
        total = total + times(piece, low_ref[pieces[part], :])
    beyond = folded(total)
    beyond_high, beyond_low = split(beyond)
    probe_high_ref[2 * points :, :] = beyond_high
    probe_low_ref[points:, :] = beyond_low
    answers = times_rows(chosen, *split(jnp.concatenate([near, near + beyond], axis=0)))
    for line in range(lines):
        rows = slice(line * TERM, (line + 1) * TERM)
        answer_ref[rows, :] = weights[line] * answers[rows]


def package_kernel(count, source_ref, retain_ref, probe_high_ref, probe_low_ref, answer_ref, shift_ref, *refs):
    starts, package_ref = refs[:count], refs[count]
    cols, width = shift_ref.shape
    points = width // 2
    start = jnp.concatenate([ref[...] for ref in starts], axis=0)
    source = jnp.concatenate([source_ref[...]] * count, axis=0)
    driven = retain_ref[...] * start + source
    chosen = probe_high_ref[:points, :]
    terms = folded(
        lax.dot_general(
            stacked(start),
            jnp.concatenate([chosen, chosen], axis=0),
            ROWS_BY_ROWS,
            preferred_element_type=f32,
        )
    )
    later = folded(times_rows(stacked(driven), probe_high_ref[points:, :], probe_low_ref[...]))
    rows = count * cols
    half = rows // 2
    lane = lax.broadcasted_iota(jnp.int32, (half, width), 1)
    package_ref[:half, :] = jnp.where(lane < points, terms[:half], terms[half:])
    package_ref[half : half + rows, :] = later + jnp.concatenate([shift_ref[...]] * count, axis=0)
    package_ref[half + rows :, :] = answer_ref[...]


def advance_kernel(count, turns, high_ref, low_ref, probe_ref, source_ref, retain_ref, *refs):
    starts = refs[:count]
    state_ref, replies_ref = refs[count:]
    points = probe_ref.shape[0] // 3
    rows = count * source_ref.shape[0]
    retain = retain_ref[...]
    source = jnp.concatenate([source_ref[...]] * count, axis=0)
    start = jnp.concatenate([ref[...] for ref in starts], axis=0)
    high, low = high_ref[...], low_ref[...]
    left = jnp.concatenate([stacked(retain * start + source), probe_ref[:points, :]], axis=0)
    out = times_rows(left, high, low)
    state = jnp.concatenate([folded(out[: 2 * rows]), out[2 * rows :]], axis=0)
    for turn in range(turns):
        replies_ref[turn * points : (turn + 1) * points, :] = state[rows:]
        driven = jnp.concatenate(
            [retain * state[:rows] + source, retain * state[rows:]], axis=0
        )
        state = folded(times_rows(stacked(driven), high, low))
    state_ref[...] = state


def finish_kernel(
    count, high_ref, low_ref, state_ref, replies_ref, source_ref, retain_ref, decay_ref, *refs
):
    starts = refs[:count]
    base_ref, reply_high_ref, reply_low_ref, partial = refs[count:]
    cols, nodes = source_ref.shape
    rows = count * cols
    points = state_ref.shape[0] - rows
    retain = retain_ref[...]
    decay = decay_ref[...]
    source = jnp.concatenate([source_ref[...]] * count, axis=0)
    state = state_ref[...]
    driven = jnp.concatenate([retain * state[:rows] + source, retain * state[rows:]], axis=0)
    final = folded(times_rows(stacked(driven), high_ref[...], low_ref[...]))
    start = jnp.concatenate([ref[...] for ref in starts], axis=0)
    partial[...] = final[:rows] - decay * start
    mine = lax.axis_index("tm")
    first = pl.ds(pl.multiple_of(mine * cols, cols), cols)
    total = partial[first, :]
    seed = starts[0][...]
    for place in range(1, count):
        seed = jnp.where(mine == place, starts[place][...], seed)
    total = total + decay * seed
    for turn in range(1, count):
        value = partial[pl.ds(pl.multiple_of((mine ^ turn) * cols, cols), cols), :]
        total = jnp.where(turn <= mine, decay * total + value, total)
    base_ref[...] = total
    reply = jnp.concatenate(
        [
            final[rows:] + state[rows:],
            jnp.zeros((points, nodes), f32),
            replies_ref[points : 2 * points, :],
            replies_ref[:points, :],
        ],
        axis=0,
    )
    reply_high_ref[...], reply_low_ref[...] = split(reply)


def last_kernel(
    subs, count, plan_ref, here_ref, there_ref, base_ref, decay_ref, reply_high_ref, reply_low_ref,
    out_ref, partial,
):
    cols, _ = base_ref.shape
    width = plan_ref.shape[1]
    points = width // 2
    rows = count * cols
    half = rows // 2
    mine = lax.axis_index("sub")
    lane = lax.broadcasted_iota(jnp.int32, (rows, width), 1)
    pairs = []
    tables = []
    for pair in range(subs // 2):
        even, odd = here_ref[pair, :half, :], there_ref[pair, :half, :]
        other_even, other_odd = pltpu.roll(even, points, 1), pltpu.roll(odd, points, 1)
        first = lane[:half] < points
        pairs.append(
            jnp.concatenate(
                [jnp.where(first, even, other_odd), jnp.where(first, other_even, odd)], axis=0
            )
        )
        tables.append(
            jnp.where(
                lane[:TERM] < points,
                here_ref[pair, half + rows + points :, :],
                there_ref[pair, half + rows + points :, :],
            )[:1]
        )
    snapshot = jnp.concatenate(pairs, axis=1)
    table = jnp.concatenate(tables, axis=1).astype(jnp.int32) ^ (mine * points)
    total = subs * points
    route = (lax.broadcasted_iota(jnp.int32, (total, total), 0) == table).astype(f32).astype(bf16)
    seen = stacked(snapshot)
    far = folded(times(seen, route))
    later = []
    for pair in range(subs // 2):
        both = far[:, pair * width : (pair + 1) * width]
        left = jnp.concatenate(
            [
                stacked(jnp.where(lane < points, both, 0.0)),
                stacked(jnp.where(lane < points, 0.0, both)),
            ],
            axis=0,
        )
        answers = jnp.concatenate(
            [
                here_ref[pair, half + rows : half + rows + points, :],
                there_ref[pair, half + rows : half + rows + points, :],
            ],
            axis=0,
        )
        high, low = split(answers)
        sums = times(left, high) + times(left, low)
        later.append(stacked(here_ref[pair, half : half + rows, :] + folded(sums[: 2 * rows])))
        later.append(stacked(there_ref[pair, half : half + rows, :] + folded(sums[2 * rows :])))
    known = jnp.concatenate(later + [seen], axis=1)
    weight = plan_ref[:1, :]
    target = plan_ref[1:2, :].astype(jnp.int32)
    pick = lax.broadcasted_iota(jnp.int32, (known.shape[1], width), 0) == target
    chosen = folded(times(known, pick.astype(f32).astype(bf16)))
    first = jnp.where(lane < points, far[:, :width], 0.0)
    left = stacked(jnp.concatenate([weight * first, weight * chosen], axis=1))
    partial[...] = folded(times(left, reply_high_ref[...]) + times(left, reply_low_ref[...]))
    decay = decay_ref[...]
    place = lax.axis_index("tm")
    total = partial[pl.ds(pl.multiple_of(place * cols, cols), cols), :]
    for turn in range(1, count):
        value = partial[pl.ds(pl.multiple_of((place ^ turn) * cols, cols), cols), :]
        total = jnp.where(turn <= place, decay * total + value, total)
    out_ref[...] = base_ref[...] + total


def exchanged(value, axis, count, flip):
    return lax.ppermute(value, axis, [(source, source ^ flip) for source in range(count)])


VMEM = pl.BlockSpec(memory_space=pltpu.VMEM)
HBM = pl.BlockSpec(memory_space=pltpu.HBM)


def shards(slices, subs, *arrays):
    return iterated(slices, subs, *arrays)


def iterated(
    slices, subs, starts, inverses, retain, sources, coarse_decay, admittance, partner,
    line_delay, line_live, term_block,
):
    cols, nodes = starts.shape[2:]
    lines = partner.shape[1]
    points = lines * TERM
    width = 2 * points
    rows = slices * cols
    start = starts.reshape(cols, nodes)
    source = sources.reshape(cols, nodes)
    inverse = inverses.reshape(nodes, nodes)
    shape = jax.ShapeDtypeStruct
    begun = [start]
    for flip in range(1, slices):
        begun.append(exchanged(start, "tm", slices, flip))
    high, low, probe_high, probe_low, answer, shift, plan = pl.pallas_call(
        functools.partial(prepare_kernel, subs),
        out_shape=(
            shape((nodes, nodes), bf16),
            shape((nodes, nodes), bf16),
            shape((3 * points, nodes), bf16),
            shape((2 * points, nodes), bf16),
            shape((points + TERM, width), f32),
            shape((cols, width), f32),
            shape((2, width), f32),
        ),
        in_specs=[HBM] * 8,
        out_specs=(VMEM,) * 7,
        scratch_shapes=[
            pltpu.SMEM((1, lines), jnp.int32),
            pltpu.SMEM((1, lines), jnp.int32),
            pltpu.SMEM((1, lines), jnp.int32),
            pltpu.SMEM((1, lines), jnp.int32),
            pltpu.SMEM((1, lines), f32),
            pltpu.VMEM((cols, nodes), f32),
            pltpu.VMEM((1, nodes), f32),
            pltpu.VMEM((nodes, nodes), f32),
            pltpu.VMEM((points, nodes), f32),
            pltpu.SemaphoreType.DMA((7,)),
            pltpu.SemaphoreType.DMA((CHUNKS,)),
            pltpu.SemaphoreType.DMA((lines,)),
        ],
        compiler_params=pltpu.CompilerParams(vmem_limit_bytes=24 << 20),
        name="prepare",
    )(
        *[
            pltpu.with_memory_space_constraint(value, pltpu.HBM)
            for value in (
                term_block, partner, line_delay, line_live, admittance, source, retain, inverse
            )
        ]
    )

    package = pl.pallas_call(
        functools.partial(package_kernel, slices),
        out_shape=shape((rows // 2 + rows + points + TERM, width), f32),
        in_specs=[VMEM] * (6 + slices),
        out_specs=VMEM,
        compiler_params=pltpu.CompilerParams(vmem_limit_bytes=16 << 20),
        name="package",
    )(source, retain, probe_high, probe_low, answer, shift, *begun)

    state, replies = pl.pallas_call(
        functools.partial(advance_kernel, slices, 2),
        out_shape=(shape((rows + points, nodes), f32), shape((2 * points, nodes), f32)),
        in_specs=[VMEM] * (5 + slices),
        out_specs=(VMEM,) * 2,
        compiler_params=pltpu.CompilerParams(vmem_limit_bytes=24 << 20),
        cost_estimate=pl.CostEstimate(
            flops=12 * nodes * nodes * 256, bytes_accessed=8 * nodes * nodes, transcendentals=0
        ),
        name="advance",
    )(high, low, probe_high, source, retain, *begun)

    here = jnp.stack(
        [package] + [exchanged(package, "sub", subs, flip) for flip in range(2, subs, 2)]
    )
    here, state = lax.optimization_barrier((here, state))
    there = exchanged(here, "sub", subs, 1)

    base, reply_high, reply_low = pl.pallas_call(
        functools.partial(finish_kernel, slices),
        out_shape=(
            shape((cols, nodes), f32),
            shape((4 * points, nodes), bf16),
            shape((4 * points, nodes), bf16),
        ),
        in_specs=[VMEM] * (7 + slices),
        out_specs=(VMEM,) * 3,
        scratch_shapes=[pltpu.VMEM((rows, nodes), f32)],
        compiler_params=pltpu.CompilerParams(vmem_limit_bytes=24 << 20),
        cost_estimate=pl.CostEstimate(
            flops=4 * nodes * nodes * 256, bytes_accessed=4 * nodes * nodes, transcendentals=0
        ),
        name="finish",
    )(high, low, state, replies, source, retain, coarse_decay, *begun)

    ends = pl.pallas_call(
        functools.partial(last_kernel, subs, slices),
        out_shape=shape((cols, nodes), f32),
        in_specs=[VMEM] * 7,
        out_specs=VMEM,
        scratch_shapes=[pltpu.VMEM((rows, nodes), f32)],
        compiler_params=pltpu.CompilerParams(vmem_limit_bytes=40 << 20),
        name="last",
    )(plan, here, there, base, coarse_decay, reply_high, reply_low)
    return ends.reshape(starts.shape)


def solution(mesh):
    return jax.shard_map(
        functools.partial(shards, mesh.shape["tm"], mesh.shape["sub"]),
        mesh=mesh,
        in_specs=(
            P("tm", "sub", None, None),
            P("sub", None, None),
            P("sub", None),
            P("sub", None, None),
            P("sub", None),
            P("sub", None),
            P("sub", None),
            P("sub", None),
            P("sub", None),
            P("sub", None),
        ),
        out_specs=P("tm", "sub", None, None),
        check_vma=False,
    )
```

```python
import functools

import jax
import jax.numpy as jnp
from jax import lax
from jax.experimental import pallas as pl
from jax.experimental.pallas import tpu as pltpu
from jax.sharding import PartitionSpec as P

TERM = 8
CHUNKS = 4

f32 = jnp.float32
bf16 = jnp.bfloat16
ROWS_BY_ROWS = (((1,), (1,)), ((), ()))


def split(value):
    high = value.astype(bf16)
    return high, (value - high.astype(f32)).astype(bf16)


def stacked(value):
    return jnp.concatenate(split(value), axis=0)


def folded(value):
    half = value.shape[0] // 2
    return value[:half] + value[half:]


def times_rows(left, high, low):
    return lax.dot_general(left, high, ROWS_BY_ROWS, preferred_element_type=f32) + lax.dot_general(
        left, low, ROWS_BY_ROWS, preferred_element_type=f32
    )


def times(left, right):
    return jnp.dot(left, right, preferred_element_type=f32)


def packs(value, count, lanes):
    half = value.shape[0] // 2
    first = lax.broadcasted_iota(jnp.int32, (half, 2 * lanes), 1) < lanes
    blocks = []
    for pair in range(count // 2):
        tile = value[:, pair * 2 * lanes : (pair + 1) * 2 * lanes]
        turned = pltpu.roll(tile, lanes, 1)
        blocks.append(jnp.where(first, tile[:half], turned[half:]))
        blocks.append(jnp.where(first, turned[:half], tile[half:]))
    return blocks


def unpacked(value):
    return jnp.concatenate([value, pltpu.roll(value, value.shape[1] // 2, 1)], axis=0)


def slot_lanes(lines, width, read):
    slot = lax.broadcasted_iota(jnp.int32, (1, width), 1) // TERM % lines
    row = jnp.full((1, width), read(0))
    for line in range(1, lines):
        row = jnp.where(slot == line, read(line), row)
    return row


def prepare_kernel(
    subs, block_hbm, partner_hbm, delay_hbm, live_hbm, admittance_hbm, source_hbm, retain_hbm,
    inverse_hbm, high_ref, low_ref, chosen_ref, probe_high_ref, probe_low_ref, answer_ref,
    shift_ref, plan_ref, scale_ref, block_ref, partner_ref, delay_ref, live_ref, admittance_ref, source_ref, retain_ref, held,
    picked, probe, landed, arrived, fetched,
):
    nodes = inverse_hbm.shape[0]
    lines = block_ref.shape[1]
    points = lines * TERM
    width = 2 * points
    depth = nodes // CHUNKS
    small = [
        pltpu.make_async_copy(source, target, landed.at[place])
        for place, (source, target) in enumerate(
            [
                (block_hbm, block_ref),
                (source_hbm, source_ref),
                (retain_hbm, retain_ref),
                (partner_hbm, partner_ref),
                (delay_hbm, delay_ref),
                (live_hbm, live_ref),
                (admittance_hbm, admittance_ref),
            ]
        )
    ]
    pieces = [pl.ds(part * depth, depth) for part in range(CHUNKS)]
    copies = [
        pltpu.make_async_copy(inverse_hbm.at[rows], held.at[rows], arrived.at[part])
        for part, rows in enumerate(pieces)
    ]
    for copy in small + copies:
        copy.start()
    small[0].wait()
    wanted = [
        pltpu.make_async_copy(
            inverse_hbm.at[pl.ds(pl.multiple_of(block_ref[0, line] * TERM, TERM), TERM)],
            picked.at[pl.ds(line * TERM, TERM)],
            fetched.at[line],
        )
        for line in range(lines)
    ]
    for copy in wanted:
        copy.start()
    offset = lax.broadcasted_iota(jnp.int32, (TERM, nodes), 1) - lax.broadcasted_iota(
        jnp.int32, (TERM, nodes), 0
    )
    chosen = jnp.concatenate(
        [(offset == block_ref[0, line] * TERM).astype(f32) for line in range(lines)], axis=0
    ).astype(bf16)
    chosen_ref[...] = chosen
    blank = jnp.zeros_like(chosen)
    probe[...] = jnp.zeros_like(probe)
    for copy in small[1:]:
        copy.wait()
    weights = [
        admittance_ref[0, line] * live_ref[0, line].astype(f32) for line in range(lines)
    ]
    mine = lax.axis_index("sub")
    room = max(1, 2 * lines // subs)
    fars = [partner_ref[0, line] for line in range(lines)]
    owners = [lax.div(far, lines) for far in fars]
    sent, wanted_rank = [], []
    for line in range(lines):
        rank = jnp.int32(0)
        before = jnp.int32(0)
        for other in range(lines):
            if other != line:
                same = owners[other] == owners[line]
                smaller = same & (fars[other] < fars[line])
                rank = rank + jnp.where(smaller, 1, 0)
            if other < line:
                before = before + jnp.where(same, 1, 0)
        block = lax.div(owners[line] ^ mine, 2)
        run = (owners[line] & 1) * room + jnp.minimum(rank, room - 1)
        sent.append(block * points + run * TERM)
        wanted_rank.append(((mine & 1) * room + jnp.minimum(before, room - 1)) * TERM)
    index = lax.broadcasted_iota(jnp.int32, (1, width), 1)
    table = slot_lanes(lines, width, lambda line: partner_ref[0, line] * TERM) + index % TERM
    place = table ^ (mine * points)
    delay = slot_lanes(lines, width, lambda line: delay_ref[0, line])
    begin = place // points * width + index % TERM
    begin = begin + slot_lanes(lines, width, lambda line: wanted_rank[line])
    early = subs * width + place
    target = jnp.where(
        index >= points,
        jnp.where(delay == 2, begin + points // 2, jnp.where(delay == 3, begin, early)),
        jnp.where(delay == 2, begin, early),
    )
    plan_ref[...] = target
    for line in range(lines):
        scale_ref[line * TERM : (line + 1) * TERM, :] = jnp.full((TERM, width), weights[line])

    def keep(part):
        copies[part].wait()
        high_ref[pieces[part], :], low_ref[pieces[part], :] = split(held[pieces[part], :])

    for part in range(CHUNKS):
        keep(part)
    for copy in wanted:
        copy.wait()
    near = picked[...]
    near_high, near_low = split(near)
    left = stacked(near * retain_ref[...])
    for line in range(lines):
        rows = pl.ds(pl.multiple_of(sent[line], TERM), TERM)
        probe[rows, :] = near[line * TERM : (line + 1) * TERM]
    spread = subs // 2 * points
    lead = lax.broadcasted_iota(jnp.int32, (TERM, spread), 1) - lax.broadcasted_iota(
        jnp.int32, (TERM, spread), 0
    )
    gather = jnp.concatenate(
        [
            (lead == sent[line] + kind * (points // 2)).astype(f32)
            for kind in range(2)
            for line in range(lines)
        ],
        axis=0,
    ).astype(bf16)
    fixed = folded(
        times_rows(
            stacked(source_ref[...]),
            jnp.concatenate([blank, near_high], axis=0),
            jnp.concatenate([blank, near_low], axis=0),
        )
    )
    shift_ref[...] = folded(times(stacked(fixed), gather))
    total = jnp.zeros((2 * points, nodes), f32)
    for part in range(CHUNKS):
        piece = left[:, part * depth : (part + 1) * depth]
        total = total + times(piece, high_ref[pieces[part], :])
        total = total + times(piece, low_ref[pieces[part], :])
    beyond = folded(total)
    for line in range(lines):
        rows = pl.ds(pl.multiple_of(sent[line] + points // 2, TERM), TERM)
        probe[rows, :] = beyond[line * TERM : (line + 1) * TERM]
    probe_high_ref[...], probe_low_ref[...] = split(probe[...])
    answers = times_rows(chosen, *split(jnp.concatenate([near, near + beyond], axis=0)))
    answers = jnp.concatenate(
        [weights[line] * answers[line * TERM : (line + 1) * TERM] for line in range(lines)], axis=0
    )
    packed = points // 2
    told = jnp.broadcast_to(table.astype(f32), (TERM, width))
    blocks = packs(folded(times(stacked(answers), gather)), subs // 2, points)
    for place, block in enumerate(blocks):
        begin = place * (packed + TERM)
        answer_ref[begin : begin + packed, :] = block
        answer_ref[begin + packed : begin + packed + TERM, :] = told


def package_kernel(
    count, blocks, source_ref, retain_ref, chosen_ref, probe_high_ref, probe_low_ref, answer_ref,
    shift_ref, *refs,
):
    starts, package_refs = refs[:count], refs[count:]
    cols = source_ref.shape[0]
    points = chosen_ref.shape[0]
    start = jnp.concatenate([ref[...] for ref in starts], axis=0)
    source = jnp.concatenate([source_ref[...]] * count, axis=0)
    driven = retain_ref[...] * start + source
    chosen = chosen_ref[...]
    terms = folded(
        lax.dot_general(
            stacked(start),
            jnp.concatenate([chosen, chosen], axis=0),
            ROWS_BY_ROWS,
            preferred_element_type=f32,
        )
    )
    later = folded(times_rows(stacked(driven), probe_high_ref[...], probe_low_ref[...]))
    later = later + jnp.concatenate([shift_ref[...]] * count, axis=0)
    half = count * cols // 2
    lane = lax.broadcasted_iota(jnp.int32, (half, 2 * points), 1)
    terms = jnp.where(lane < points, terms[:half], terms[half:])
    depth = answer_ref.shape[0] // blocks
    for place, block in enumerate(packs(later, blocks, points)):
        package_refs[place][:half, :] = terms
        package_refs[place][half : 2 * half, :] = block
        package_refs[place][2 * half :, :] = answer_ref[place * depth : (place + 1) * depth, :]


def advance_kernel(count, turns, high_ref, low_ref, chosen_ref, scale_ref, source_ref, retain_ref, *refs):
    starts = refs[:count]
    state_ref, reply_high_ref, reply_low_ref = refs[count:]
    points = chosen_ref.shape[0]
    rows = count * source_ref.shape[0]
    retain = retain_ref[...]
    source = jnp.concatenate([source_ref[...]] * count, axis=0)
    start = jnp.concatenate([ref[...] for ref in starts], axis=0)
    high, low = high_ref[...], low_ref[...]
    left = jnp.concatenate([stacked(retain * start + source), chosen_ref[...]], axis=0)
    out = times_rows(left, high, low)
    scale = jnp.concatenate([scale_ref[...]] * (out.shape[1] // scale_ref.shape[1]), axis=1)
    state = jnp.concatenate([folded(out[: 2 * rows]), scale * out[2 * rows :]], axis=0)
    for turn in range(turns):
        kept = slice((turns - 1 - turn) * points, (turns - turn) * points)
        reply_high_ref[kept, :], reply_low_ref[kept, :] = split(state[rows:])
        driven = jnp.concatenate(
            [retain * state[:rows] + source, retain * state[rows:]], axis=0
        )
        state = folded(times_rows(stacked(driven), high, low))
    state_ref[...] = state


def finish_kernel(
    count, high_ref, low_ref, state_ref, later_high_ref, later_low_ref, source_ref, retain_ref,
    decay_ref, *refs,
):
    starts = refs[:count]
    base_ref, reply_high_ref, reply_low_ref, partial = refs[count:]
    cols, _ = source_ref.shape
    rows = count * cols
    points = state_ref.shape[0] - rows
    retain = retain_ref[...]
    decay = decay_ref[...]
    source = jnp.concatenate([source_ref[...]] * count, axis=0)
    state = state_ref[...]
    driven = jnp.concatenate([retain * state[:rows] + source, retain * state[rows:]], axis=0)
    final = folded(times_rows(stacked(driven), high_ref[...], low_ref[...]))
    start = jnp.concatenate([ref[...] for ref in starts], axis=0)
    partial[...] = final[:rows] - decay * start
    mine = lax.axis_index("tm")
    first = pl.ds(pl.multiple_of(mine * cols, cols), cols)
    total = partial[first, :]
    seed = starts[0][...]
    for place in range(1, count):
        seed = jnp.where(mine == place, starts[place][...], seed)
    total = total + decay * seed
    for turn in range(1, count):
        value = partial[pl.ds(pl.multiple_of((mine ^ turn) * cols, cols), cols), :]
        total = jnp.where(turn <= mine, decay * total + value, total)
    base_ref[...] = total
    high, low = split(final[rows:] + state[rows:])
    blank = jnp.zeros_like(high)
    for target, first, later in (
        (reply_high_ref, high, later_high_ref),
        (reply_low_ref, low, later_low_ref),
    ):
        target[:points, :] = first
        target[points : 2 * points, :] = blank
        target[2 * points :, :] = later[...]


def last_kernel(
    subs, count, plan_ref, here_ref, there_ref, base_ref, decay_ref, reply_high_ref, reply_low_ref,
    out_ref, partial,
):
    cols, _ = base_ref.shape
    width = plan_ref.shape[1]
    points = width // 2
    rows = count * cols
    half = rows // 2
    mine = lax.axis_index("sub")
    lane = lax.broadcasted_iota(jnp.int32, (rows, width), 1)
    pairs = []
    tables = []
    for pair in range(subs // 2):
        even, odd = here_ref[pair, :half, :], there_ref[pair, :half, :]
        other_even, other_odd = pltpu.roll(even, points, 1), pltpu.roll(odd, points, 1)
        first = lane[:half] < points
        pairs.append(
            jnp.concatenate(
                [jnp.where(first, even, other_odd), jnp.where(first, other_even, odd)], axis=0
            )
        )
        tables.append(
            jnp.where(
                lane[:TERM] < points,
                here_ref[pair, rows + points // 2 :, :],
                there_ref[pair, rows + points // 2 :, :],
            )[:1]
        )
    snapshot = jnp.concatenate(pairs, axis=1)
    table = jnp.concatenate(tables, axis=1).astype(jnp.int32) ^ (mine * points)
    total = subs * points
    route = (lax.broadcasted_iota(jnp.int32, (total, total), 0) == table).astype(f32).astype(bf16)
    seen = stacked(snapshot)
    far = times(seen, route)
    lane = jnp.concatenate([lane, lane], axis=0)
    later = []
    for pair in range(subs // 2):
        both = far[:, pair * width : (pair + 1) * width]
        left = jnp.concatenate(
            [jnp.where(lane < points, both, 0.0), jnp.where(lane < points, 0.0, both)], axis=0
        ).astype(bf16)
        answers = jnp.concatenate(
            [
                unpacked(here_ref[pair, rows : rows + points // 2, :]),
                unpacked(there_ref[pair, rows : rows + points // 2, :]),
            ],
            axis=0,
        )
        high, low = split(answers)
        sums = times(left, high) + times(left, low)
        later.append(stacked(unpacked(here_ref[pair, half:rows, :]) + folded(sums[: 2 * rows])))
        later.append(stacked(unpacked(there_ref[pair, half:rows, :]) + folded(sums[2 * rows :])))
    known = jnp.concatenate(later + [seen], axis=1)
    pick = lax.broadcasted_iota(jnp.int32, (known.shape[1], width), 0) == plan_ref[...]
    chosen = times(known, pick.astype(f32).astype(bf16))
    first = jnp.where(lane < points, far[:, :width], 0.0)
    left = jnp.concatenate([first, chosen], axis=1).astype(bf16)
    partial[...] = folded(times(left, reply_high_ref[...]) + times(left, reply_low_ref[...]))
    decay = decay_ref[...]
    place = lax.axis_index("tm")
    total = partial[pl.ds(pl.multiple_of(place * cols, cols), cols), :]
    for turn in range(1, count):
        value = partial[pl.ds(pl.multiple_of((place ^ turn) * cols, cols), cols), :]
        total = jnp.where(turn <= place, decay * total + value, total)
    out_ref[...] = base_ref[...] + total


def exchanged(value, axis, count, flip):
    return lax.ppermute(value, axis, [(source, source ^ flip) for source in range(count)])


VMEM = pl.BlockSpec(memory_space=pltpu.VMEM)
HBM = pl.BlockSpec(memory_space=pltpu.HBM)


def shards(slices, subs, *arrays):
    return iterated(slices, subs, *arrays)


def iterated(
    slices, subs, starts, inverses, retain, sources, coarse_decay, admittance, partner,
    line_delay, line_live, term_block,
):
    cols, nodes = starts.shape[2:]
    lines = partner.shape[1]
    points = lines * TERM
    width = 2 * points
    rows = slices * cols
    start = starts.reshape(cols, nodes)
    source = sources.reshape(cols, nodes)
    inverse = inverses.reshape(nodes, nodes)
    shape = jax.ShapeDtypeStruct
    begun = [start]
    for flip in range(1, slices):
        begun.append(exchanged(start, "tm", slices, flip))
    blocks = subs // 2
    spread = blocks * points
    high, low, chosen, probe_high, probe_low, answer, shift, plan, scale = pl.pallas_call(
        functools.partial(prepare_kernel, subs),
        out_shape=(
            shape((nodes, nodes), bf16),
            shape((nodes, nodes), bf16),
            shape((points, nodes), bf16),
            shape((spread, nodes), bf16),
            shape((spread, nodes), bf16),
            shape((blocks * (points // 2 + TERM), width), f32),
            shape((cols, spread), f32),
            shape((1, width), jnp.int32),
            shape((points, width), f32),
        ),
        in_specs=[HBM] * 8,
        out_specs=(VMEM,) * 9,
        scratch_shapes=[
            pltpu.SMEM((1, lines), jnp.int32),
            pltpu.SMEM((1, lines), jnp.int32),
            pltpu.SMEM((1, lines), jnp.int32),
            pltpu.SMEM((1, lines), jnp.int32),
            pltpu.SMEM((1, lines), f32),
            pltpu.VMEM((cols, nodes), f32),
            pltpu.VMEM((1, nodes), f32),
            pltpu.VMEM((nodes, nodes), f32),
            pltpu.VMEM((points, nodes), f32),
            pltpu.VMEM((spread, nodes), f32),
            pltpu.SemaphoreType.DMA((7,)),
            pltpu.SemaphoreType.DMA((CHUNKS,)),
            pltpu.SemaphoreType.DMA((lines,)),
        ],
        compiler_params=pltpu.CompilerParams(vmem_limit_bytes=24 << 20),
        name="prepare",
    )(
        *[
            pltpu.with_memory_space_constraint(value, pltpu.HBM)
            for value in (
                term_block, partner, line_delay, line_live, admittance, source, retain, inverse
            )
        ]
    )

    packages = pl.pallas_call(
        functools.partial(package_kernel, slices, blocks),
        out_shape=(shape((rows + points // 2 + TERM, width), f32),) * blocks,
        in_specs=[VMEM] * (7 + slices),
        out_specs=(VMEM,) * blocks,
        compiler_params=pltpu.CompilerParams(vmem_limit_bytes=16 << 20),
        name="package",
    )(source, retain, chosen, probe_high, probe_low, answer, shift, *begun)

    state, later_high, later_low = pl.pallas_call(
        functools.partial(advance_kernel, slices, 2),
        out_shape=(
            shape((rows + points, nodes), f32),
            shape((2 * points, nodes), bf16),
            shape((2 * points, nodes), bf16),
        ),
        in_specs=[VMEM] * (6 + slices),
        out_specs=(VMEM,) * 3,
        compiler_params=pltpu.CompilerParams(vmem_limit_bytes=24 << 20),
        cost_estimate=pl.CostEstimate(
            flops=12 * nodes * nodes * 256, bytes_accessed=8 * nodes * nodes, transcendentals=0
        ),
        name="advance",
    )(high, low, chosen, scale, source, retain, *begun)

    gathered = [packages[0]]
    for flip in range(2, subs, 2):
        gathered.append(exchanged(packages[flip // 2], "sub", subs, flip))
    here = jnp.stack(gathered)
    here, state = lax.optimization_barrier((here, state))
    there = exchanged(here, "sub", subs, 1)

    base, reply_high, reply_low = pl.pallas_call(
        functools.partial(finish_kernel, slices),
        out_shape=(
            shape((cols, nodes), f32),
            shape((4 * points, nodes), bf16),
            shape((4 * points, nodes), bf16),
        ),
        in_specs=[VMEM] * (8 + slices),
        out_specs=(VMEM,) * 3,
        scratch_shapes=[pltpu.VMEM((rows, nodes), f32)],
        compiler_params=pltpu.CompilerParams(vmem_limit_bytes=24 << 20),
        cost_estimate=pl.CostEstimate(
            flops=4 * nodes * nodes * 256, bytes_accessed=4 * nodes * nodes, transcendentals=0
        ),
        name="finish",
    )(high, low, state, later_high, later_low, source, retain, coarse_decay, *begun)

    ends = pl.pallas_call(
        functools.partial(last_kernel, subs, slices),
        out_shape=shape((cols, nodes), f32),
        in_specs=[VMEM] * 7,
        out_specs=VMEM,
        scratch_shapes=[pltpu.VMEM((rows, nodes), f32)],
        compiler_params=pltpu.CompilerParams(vmem_limit_bytes=40 << 20),
        name="last",
    )(plan, here, there, base, coarse_decay, reply_high, reply_low)
    return ends.reshape(starts.shape)


def solution(mesh):
    return jax.shard_map(
        functools.partial(shards, mesh.shape["tm"], mesh.shape["sub"]),
        mesh=mesh,
        in_specs=(
            P("tm", "sub", None, None),
            P("sub", None, None),
            P("sub", None),
            P("sub", None, None),
            P("sub", None),
            P("sub", None),
            P("sub", None),
            P("sub", None),
            P("sub", None),
            P("sub", None),
        ),
        out_specs=P("tm", "sub", None, None),
        check_vma=False,
    )
```

```python
import functools

import jax
import jax.numpy as jnp
from jax import lax
from jax.experimental import pallas as pl
from jax.experimental.pallas import tpu as pltpu
from jax.sharding import PartitionSpec as P

TERM = 8
CHUNKS = 4

f32 = jnp.float32
bf16 = jnp.bfloat16
ROWS_BY_ROWS = (((1,), (1,)), ((), ()))


def split(value):
    high = value.astype(bf16)
    return high, (value - high.astype(f32)).astype(bf16)


def stacked(value):
    return jnp.concatenate(split(value), axis=0)


def folded(value):
    half = value.shape[0] // 2
    return value[:half] + value[half:]


def times_rows(left, high, low):
    return lax.dot_general(left, high, ROWS_BY_ROWS, preferred_element_type=f32) + lax.dot_general(
        left, low, ROWS_BY_ROWS, preferred_element_type=f32
    )


def times(left, right):
    return jnp.dot(left, right, preferred_element_type=f32)


def packs(value, count, lanes):
    half = value.shape[0] // 2
    first = lax.broadcasted_iota(jnp.int32, (half, 2 * lanes), 1) < lanes
    blocks = []
    for pair in range(count // 2):
        tile = value[:, pair * 2 * lanes : (pair + 1) * 2 * lanes]
        turned = pltpu.roll(tile, lanes, 1)
        blocks.append(jnp.where(first, tile[:half], turned[half:]))
        blocks.append(jnp.where(first, turned[:half], tile[half:]))
    return blocks


def unpacked(value):
    return jnp.concatenate([value, pltpu.roll(value, value.shape[1] // 2, 1)], axis=0)


def slot_lanes(lines, width, read):
    slot = lax.broadcasted_iota(jnp.int32, (1, width), 1) // TERM % lines
    row = jnp.full((1, width), read(0))
    for line in range(1, lines):
        row = jnp.where(slot == line, read(line), row)
    return row


def prepare_kernel(
    subs, block_hbm, partner_hbm, delay_hbm, live_hbm, admittance_hbm, source_hbm, retain_hbm,
    inverse_hbm, high_ref, low_ref, chosen_ref, probe_high_ref, probe_low_ref, answer_ref,
    shift_ref, plan_ref, scale_ref, block_ref, partner_ref, delay_ref, live_ref, admittance_ref, source_ref, retain_ref, held,
    picked, probe, landed, arrived, fetched,
):
    nodes = inverse_hbm.shape[0]
    lines = block_ref.shape[1]
    points = lines * TERM
    width = 2 * points
    depth = nodes // CHUNKS
    small = [
        pltpu.make_async_copy(source, target, landed.at[place])
        for place, (source, target) in enumerate(
            [
                (block_hbm, block_ref),
                (source_hbm, source_ref),
                (retain_hbm, retain_ref),
                (partner_hbm, partner_ref),
                (delay_hbm, delay_ref),
                (live_hbm, live_ref),
                (admittance_hbm, admittance_ref),
            ]
        )
    ]
    pieces = [pl.ds(part * depth, depth) for part in range(CHUNKS)]
    copies = [
        pltpu.make_async_copy(inverse_hbm.at[rows], held.at[rows], arrived.at[part])
        for part, rows in enumerate(pieces)
    ]
    for copy in small + copies:
        copy.start()
    small[0].wait()
    wanted = [
        pltpu.make_async_copy(
            inverse_hbm.at[pl.ds(pl.multiple_of(block_ref[0, line] * TERM, TERM), TERM)],
            picked.at[pl.ds(line * TERM, TERM)],
            fetched.at[line],
        )
        for line in range(lines)
    ]
    for copy in wanted:
        copy.start()
    offset = lax.broadcasted_iota(jnp.int32, (TERM, nodes), 1) - lax.broadcasted_iota(
        jnp.int32, (TERM, nodes), 0
    )
    chosen = jnp.concatenate(
        [(offset == block_ref[0, line] * TERM).astype(f32) for line in range(lines)], axis=0
    ).astype(bf16)
    chosen_ref[...] = chosen
    blank = jnp.zeros_like(chosen)
    probe[...] = jnp.zeros_like(probe)
    for copy in small[1:]:
        copy.wait()
    weights = [
        admittance_ref[0, line] * live_ref[0, line].astype(f32) for line in range(lines)
    ]
    mine = lax.axis_index("sub")
    room = max(1, 2 * lines // subs)
    fars = [partner_ref[0, line] for line in range(lines)]
    owners = [lax.div(far, lines) for far in fars]
    sent, wanted_rank = [], []
    for line in range(lines):
        rank = jnp.int32(0)
        before = jnp.int32(0)
        for other in range(lines):
            if other != line:
                same = owners[other] == owners[line]
                smaller = same & (fars[other] < fars[line])
                rank = rank + jnp.where(smaller, 1, 0)
            if other < line:
                before = before + jnp.where(same, 1, 0)
        block = lax.div(owners[line] ^ mine, 2)
        run = (owners[line] & 1) * room + jnp.minimum(rank, room - 1)
        sent.append(block * points + run * TERM)
        wanted_rank.append(((mine & 1) * room + jnp.minimum(before, room - 1)) * TERM)
    index = lax.broadcasted_iota(jnp.int32, (1, width), 1)
    table = slot_lanes(lines, width, lambda line: partner_ref[0, line] * TERM) + index % TERM
    place = table ^ (mine * points)
    delay = slot_lanes(lines, width, lambda line: delay_ref[0, line])
    begin = subs * points + place // points * width + index % TERM
    begin = begin + slot_lanes(lines, width, lambda line: wanted_rank[line])
    early = place
    target = jnp.where(
        index >= points,
        jnp.where(delay == 2, begin + points // 2, jnp.where(delay == 3, begin, early)),
        jnp.where(delay == 2, begin, early),
    )
    plan_ref[...] = target
    for line in range(lines):
        scale_ref[line * TERM : (line + 1) * TERM, :] = jnp.full((TERM, width), weights[line])

    def keep(part):
        copies[part].wait()
        high_ref[pieces[part], :], low_ref[pieces[part], :] = split(held[pieces[part], :])

    for part in range(CHUNKS):
        keep(part)
    for copy in wanted:
        copy.wait()
    near = picked[...]
    near_high, near_low = split(near)
    left = stacked(near * retain_ref[...])
    for line in range(lines):
        rows = pl.ds(pl.multiple_of(sent[line], TERM), TERM)
        probe[rows, :] = near[line * TERM : (line + 1) * TERM]
    spread = subs // 2 * points
    lead = lax.broadcasted_iota(jnp.int32, (TERM, spread), 1) - lax.broadcasted_iota(
        jnp.int32, (TERM, spread), 0
    )
    gather = jnp.concatenate(
        [
            (lead == sent[line] + kind * (points // 2)).astype(f32)
            for kind in range(2)
            for line in range(lines)
        ],
        axis=0,
    ).astype(bf16)
    fixed = folded(
        times_rows(
            stacked(source_ref[...]),
            jnp.concatenate([blank, near_high], axis=0),
            jnp.concatenate([blank, near_low], axis=0),
        )
    )
    shift_ref[...] = folded(times(stacked(fixed), gather))
    total = jnp.zeros((2 * points, nodes), f32)
    for part in range(CHUNKS):
        piece = left[:, part * depth : (part + 1) * depth]
        total = total + times(piece, high_ref[pieces[part], :])
        total = total + times(piece, low_ref[pieces[part], :])
    beyond = folded(total)
    for line in range(lines):
        rows = pl.ds(pl.multiple_of(sent[line] + points // 2, TERM), TERM)
        probe[rows, :] = beyond[line * TERM : (line + 1) * TERM]
    probe_high_ref[...], probe_low_ref[...] = split(probe[...])
    answers = times_rows(chosen, *split(jnp.concatenate([near, near + beyond], axis=0)))
    answers = jnp.concatenate(
        [weights[line] * answers[line * TERM : (line + 1) * TERM] for line in range(lines)], axis=0
    )
    packed = points // 2
    told = jnp.broadcast_to(table.astype(f32), (TERM, width))
    blocks = packs(folded(times(stacked(answers), gather)), subs // 2, points)
    for place, block in enumerate(blocks):
        begin = place * (packed + TERM)
        answer_ref[begin : begin + packed, :] = block
        answer_ref[begin + packed : begin + packed + TERM, :] = told


def package_kernel(
    count, blocks, source_ref, retain_ref, chosen_ref, probe_high_ref, probe_low_ref, answer_ref,
    shift_ref, *refs,
):
    starts, package_refs = refs[:count], refs[count:]
    cols = source_ref.shape[0]
    points = chosen_ref.shape[0]
    start = jnp.concatenate([ref[...] for ref in starts], axis=0)
    source = jnp.concatenate([source_ref[...]] * count, axis=0)
    driven = retain_ref[...] * start + source
    chosen = chosen_ref[...]
    later = folded(times_rows(stacked(driven), probe_high_ref[...], probe_low_ref[...]))
    later = later + jnp.concatenate([shift_ref[...]] * count, axis=0)
    half = count * cols // 2
    depth = answer_ref.shape[0] // blocks
    for place, block in enumerate(packs(later, blocks, points)):
        package_refs[place][half : 2 * half, :] = block
        package_refs[place][2 * half :, :] = answer_ref[place * depth : (place + 1) * depth, :]
    terms = folded(
        lax.dot_general(
            stacked(start), chosen, ROWS_BY_ROWS, preferred_element_type=f32
        )
    )
    terms = jnp.concatenate([terms[:half], terms[half:]], axis=1)
    for ref in package_refs:
        ref[:half, :] = terms


def advance_kernel(count, turns, high_ref, low_ref, chosen_ref, scale_ref, source_ref, retain_ref, *refs):
    starts = refs[:count]
    state_ref, reply_high_ref, reply_low_ref = refs[count:]
    points = chosen_ref.shape[0]
    rows = count * source_ref.shape[0]
    retain = retain_ref[...]
    source = jnp.concatenate([source_ref[...]] * count, axis=0)
    start = jnp.concatenate([ref[...] for ref in starts], axis=0)
    high, low = high_ref[...], low_ref[...]
    left = jnp.concatenate([stacked(retain * start + source), chosen_ref[...]], axis=0)
    out = times_rows(left, high, low)
    scale = jnp.concatenate([scale_ref[...]] * (out.shape[1] // scale_ref.shape[1]), axis=1)
    state = jnp.concatenate([folded(out[: 2 * rows]), scale * out[2 * rows :]], axis=0)
    for turn in range(turns):
        kept = slice((turns - 1 - turn) * points, (turns - turn) * points)
        reply_high_ref[kept, :], reply_low_ref[kept, :] = split(state[rows:])
        driven = jnp.concatenate(
            [retain * state[:rows] + source, retain * state[rows:]], axis=0
        )
        state = folded(times_rows(stacked(driven), high, low))
    state_ref[...] = state


def finish_kernel(
    count, high_ref, low_ref, state_ref, later_high_ref, later_low_ref, source_ref, retain_ref,
    decay_ref, *refs,
):
    starts = refs[:count]
    base_ref, reply_high_ref, reply_low_ref, partial = refs[count:]
    cols, _ = source_ref.shape
    rows = count * cols
    points = state_ref.shape[0] - rows
    retain = retain_ref[...]
    decay = decay_ref[...]
    source = jnp.concatenate([source_ref[...]] * count, axis=0)
    state = state_ref[...]
    driven = jnp.concatenate([retain * state[:rows] + source, retain * state[rows:]], axis=0)
    final = folded(times_rows(stacked(driven), high_ref[...], low_ref[...]))
    start = jnp.concatenate([ref[...] for ref in starts], axis=0)
    partial[...] = final[:rows] - decay * start
    mine = lax.axis_index("tm")
    first = pl.ds(pl.multiple_of(mine * cols, cols), cols)
    total = partial[first, :]
    seed = starts[0][...]
    for place in range(1, count):
        seed = jnp.where(mine == place, starts[place][...], seed)
    total = total + decay * seed
    for turn in range(1, count):
        value = partial[pl.ds(pl.multiple_of((mine ^ turn) * cols, cols), cols), :]
        total = jnp.where(turn <= mine, decay * total + value, total)
    base_ref[...] = total
    high, low = split(final[rows:] + state[rows:])
    blank = jnp.zeros_like(high)
    for target, first, later in (
        (reply_high_ref, high, later_high_ref),
        (reply_low_ref, low, later_low_ref),
    ):
        target[:points, :] = first
        target[points : 2 * points, :] = blank
        target[2 * points :, :] = later[...]


def last_kernel(
    subs, count, plan_ref, here_ref, there_ref, base_ref, decay_ref, reply_high_ref, reply_low_ref,
    out_ref, partial,
):
    cols, _ = base_ref.shape
    width = plan_ref.shape[1]
    points = width // 2
    rows = count * cols
    half = rows // 2
    mine = lax.axis_index("sub")
    lane = lax.broadcasted_iota(jnp.int32, (rows, width), 1)
    pairs = []
    tables = []
    for pair in range(subs // 2):
        even, odd = here_ref[pair, :half, :], there_ref[pair, :half, :]
        other_even, other_odd = pltpu.roll(even, points, 1), pltpu.roll(odd, points, 1)
        first = lane[:half] < points
        pairs.append(
            jnp.concatenate(
                [jnp.where(first, even, other_odd), jnp.where(first, other_even, odd)], axis=0
            )
        )
        tables.append(
            jnp.where(
                lane[:TERM] < points,
                here_ref[pair, rows + points // 2 :, :],
                there_ref[pair, rows + points // 2 :, :],
            )[:1]
        )
    snapshot = jnp.concatenate(pairs, axis=1)
    table = jnp.concatenate(tables, axis=1).astype(jnp.int32) ^ (mine * points)
    total = subs * points
    route = (lax.broadcasted_iota(jnp.int32, (total, total), 0) == table).astype(f32).astype(bf16)
    seen = stacked(snapshot)
    far = times(seen, route)
    lane = jnp.concatenate([lane, lane], axis=0)
    later = []
    for pair in range(subs // 2):
        both = far[:, pair * width : (pair + 1) * width]
        left = jnp.concatenate(
            [jnp.where(lane < points, both, 0.0), jnp.where(lane < points, 0.0, both)], axis=0
        ).astype(bf16)
        answers = jnp.concatenate(
            [
                unpacked(here_ref[pair, rows : rows + points // 2, :]),
                unpacked(there_ref[pair, rows : rows + points // 2, :]),
            ],
            axis=0,
        )
        high, low = split(answers)
        sums = times(left, high) + times(left, low)
        later.append(stacked(unpacked(here_ref[pair, half:rows, :]) + folded(sums[: 2 * rows])))
        later.append(stacked(unpacked(there_ref[pair, half:rows, :]) + folded(sums[2 * rows :])))
    known = jnp.concatenate([seen] + later, axis=1)
    pick = lax.broadcasted_iota(jnp.int32, (known.shape[1], width), 0) == plan_ref[...]
    chosen = times(known, pick.astype(f32).astype(bf16))
    first = jnp.where(lane < points, far[:, :width], 0.0)
    left = jnp.concatenate([first, chosen], axis=1).astype(bf16)
    partial[...] = folded(times(left, reply_high_ref[...]) + times(left, reply_low_ref[...]))
    decay = decay_ref[...]
    place = lax.axis_index("tm")
    total = partial[pl.ds(pl.multiple_of(place * cols, cols), cols), :]
    for turn in range(1, count):
        value = partial[pl.ds(pl.multiple_of((place ^ turn) * cols, cols), cols), :]
        total = jnp.where(turn <= place, decay * total + value, total)
    out_ref[...] = base_ref[...] + total


def exchanged(value, axis, count, flip):
    return lax.ppermute(value, axis, [(source, source ^ flip) for source in range(count)])


VMEM = pl.BlockSpec(memory_space=pltpu.VMEM)
HBM = pl.BlockSpec(memory_space=pltpu.HBM)


def shards(slices, subs, *arrays):
    return iterated(slices, subs, *arrays)


def iterated(
    slices, subs, starts, inverses, retain, sources, coarse_decay, admittance, partner,
    line_delay, line_live, term_block,
):
    cols, nodes = starts.shape[2:]
    lines = partner.shape[1]
    points = lines * TERM
    width = 2 * points
    rows = slices * cols
    start = starts.reshape(cols, nodes)
    source = sources.reshape(cols, nodes)
    inverse = inverses.reshape(nodes, nodes)
    shape = jax.ShapeDtypeStruct
    begun = [start]
    for flip in range(1, slices):
        begun.append(exchanged(start, "tm", slices, flip))
    blocks = subs // 2
    spread = blocks * points
    high, low, chosen, probe_high, probe_low, answer, shift, plan, scale = pl.pallas_call(
        functools.partial(prepare_kernel, subs),
        out_shape=(
            shape((nodes, nodes), bf16),
            shape((nodes, nodes), bf16),
            shape((points, nodes), bf16),
            shape((spread, nodes), bf16),
            shape((spread, nodes), bf16),
            shape((blocks * (points // 2 + TERM), width), f32),
            shape((cols, spread), f32),
            shape((1, width), jnp.int32),
            shape((points, width), f32),
        ),
        in_specs=[HBM] * 8,
        out_specs=(VMEM,) * 9,
        scratch_shapes=[
            pltpu.SMEM((1, lines), jnp.int32),
            pltpu.SMEM((1, lines), jnp.int32),
            pltpu.SMEM((1, lines), jnp.int32),
            pltpu.SMEM((1, lines), jnp.int32),
            pltpu.SMEM((1, lines), f32),
            pltpu.VMEM((cols, nodes), f32),
            pltpu.VMEM((1, nodes), f32),
            pltpu.VMEM((nodes, nodes), f32),
            pltpu.VMEM((points, nodes), f32),
            pltpu.VMEM((spread, nodes), f32),
            pltpu.SemaphoreType.DMA((7,)),
            pltpu.SemaphoreType.DMA((CHUNKS,)),
            pltpu.SemaphoreType.DMA((lines,)),
        ],
        compiler_params=pltpu.CompilerParams(vmem_limit_bytes=24 << 20),
        name="prepare",
    )(
        *[
            pltpu.with_memory_space_constraint(value, pltpu.HBM)
            for value in (
                term_block, partner, line_delay, line_live, admittance, source, retain, inverse
            )
        ]
    )

    packages = pl.pallas_call(
        functools.partial(package_kernel, slices, blocks),
        out_shape=(shape((rows + points // 2 + TERM, width), f32),) * blocks,
        in_specs=[VMEM] * (7 + slices),
        out_specs=(VMEM,) * blocks,
        compiler_params=pltpu.CompilerParams(vmem_limit_bytes=16 << 20),
        name="package",
    )(source, retain, chosen, probe_high, probe_low, answer, shift, *begun)

    state, later_high, later_low = pl.pallas_call(
        functools.partial(advance_kernel, slices, 2),
        out_shape=(
            shape((rows + points, nodes), f32),
            shape((2 * points, nodes), bf16),
            shape((2 * points, nodes), bf16),
        ),
        in_specs=[VMEM] * (6 + slices),
        out_specs=(VMEM,) * 3,
        compiler_params=pltpu.CompilerParams(vmem_limit_bytes=24 << 20),
        cost_estimate=pl.CostEstimate(
            flops=12 * nodes * nodes * 256, bytes_accessed=8 * nodes * nodes, transcendentals=0
        ),
        name="advance",
    )(high, low, chosen, scale, source, retain, *begun)

    gathered = [packages[0]]
    for flip in range(2, subs, 2):
        gathered.append(exchanged(packages[flip // 2], "sub", subs, flip))
    here = jnp.stack(gathered)
    here, state = lax.optimization_barrier((here, state))
    there = exchanged(here, "sub", subs, 1)

    base, reply_high, reply_low = pl.pallas_call(
        functools.partial(finish_kernel, slices),
        out_shape=(
            shape((cols, nodes), f32),
            shape((4 * points, nodes), bf16),
            shape((4 * points, nodes), bf16),
        ),
        in_specs=[VMEM] * (8 + slices),
        out_specs=(VMEM,) * 3,
        scratch_shapes=[pltpu.VMEM((rows, nodes), f32)],
        compiler_params=pltpu.CompilerParams(vmem_limit_bytes=24 << 20),
        cost_estimate=pl.CostEstimate(
            flops=4 * nodes * nodes * 256, bytes_accessed=4 * nodes * nodes, transcendentals=0
        ),
        name="finish",
    )(high, low, state, later_high, later_low, source, retain, coarse_decay, *begun)

    ends = pl.pallas_call(
        functools.partial(last_kernel, subs, slices),
        out_shape=shape((cols, nodes), f32),
        in_specs=[VMEM] * 7,
        out_specs=VMEM,
        scratch_shapes=[pltpu.VMEM((rows, nodes), f32)],
        compiler_params=pltpu.CompilerParams(vmem_limit_bytes=40 << 20),
        name="last",
    )(plan, here, there, base, coarse_decay, reply_high, reply_low)
    return ends.reshape(starts.shape)


def solution(mesh):
    return jax.shard_map(
        functools.partial(shards, mesh.shape["tm"], mesh.shape["sub"]),
        mesh=mesh,
        in_specs=(
            P("tm", "sub", None, None),
            P("sub", None, None),
            P("sub", None),
            P("sub", None, None),
            P("sub", None),
            P("sub", None),
            P("sub", None),
            P("sub", None),
            P("sub", None),
            P("sub", None),
        ),
        out_specs=P("tm", "sub", None, None),
        check_vma=False,
    )
```
